128 devices in a mesh: dom: 128 (over x, y, z, core).
Axes of the slice: x: 4, y: 4, z: 4, core: 2. Of those that a mesh axis runs over, the one named last changes fastest.
Arguments:
- ham_core: float32 [81920, 1280], P('dom')
- halo_rows: float32 [128, 8, 80, 1280], P('dom'), as said below
- halo_request: int32 [128, 160], P('dom'), may hold values from -1 to 159, as said below
- deriv: float32 [3, 20480, 4, 1280], P(None, 'dom'), may hold values from -15 to 15
- e_low: float32 [1], replicated, may hold values from -8 to -5
- e_high: float32 [1], replicated, may hold values from 4.5 to 7.5
- branches: int32 [5], replicated, may hold values from 0 to 1
Outputs:
- density: float32 [81920, 1280], P('dom')
- forces: float32 [3, 20480], P(None, 'dom')
The draws below stay inside these ranges and needn't reach their ends.
Inputs may be any that keep to these rules, and one draw needn't show every extreme that they name: Entry halo_request[d, k * 20 + s] is an atom index of the owner of block k of d, or -1 for an empty slot; in each block of 20 the live entries come first and are distinct; in every draw some partition asks 20 atoms of each of its 8 neighbours and is asked 20 atoms by each of them. For c < 640: halo_rows[p, k, r, c] equals ham_core[d * 640 + c, 640 + 4 * 20 * k + r] with d = (p - off_k) mod 128.
All inputs are finite; a program needn't handle non-finite values.
Results may differ from the reference program's by a relative error of at most 0.0003.
Values sent between devices are 32-bit elements; how exact they have to be, the bound alone decides.
A program may use at most 128 MiB of HBM per device.

```python
import jax
import jax.numpy as jnp
from jax import lax

ORB = 4
ATOM_DEV = 160
NB = 4
CAP = 20
ITERS = 5
ROWS = 640
HALO_SLOTS = 160
ATOM_S = 320
M = 1280
ATOMS = 20480
NORB = 81920
N_DOM = 128


def neighbour_offsets_drawn():
    blocks = jnp.arange(2 * NB, dtype=jnp.int32)
    return jnp.where(blocks < NB, blocks + 1, NB - 1 - blocks).astype(jnp.int32)


def onsite_values(key, orbital):
    low_key, high_key = jax.random.split(key)
    s_level = jax.random.uniform(low_key, orbital.shape, jnp.float32, -2.5, -1.5)
    p_level = jax.random.uniform(high_key, orbital.shape, jnp.float32, 0.5, 1.5)
    return jnp.where(orbital % ORB == 0, s_level, p_level)


def coupling(key, block_shape):
    spread = 1.2 * M ** (-0.5)
    return jax.random.normal(key, block_shape, jnp.float32) * spread


def core_hamiltonian(key):
    base_key = jax.random.fold_in(key, 11)
    values = coupling(jax.random.fold_in(base_key, 1), (NORB, M))
    row_ids = lax.broadcasted_iota(jnp.int32, (NORB, M), 0)
    col_ids = lax.broadcasted_iota(jnp.int32, (NORB, M), 1)
    levels = onsite_values(jax.random.fold_in(base_key, 2), row_ids[:, :1])
    return jnp.where(col_ids == row_ids % ROWS, levels, values)


def draw_ham_core(key, part):
    return core_hamiltonian(key)


def draw_halo_rows(key, part):
    devices = NORB // ROWS
    blocks = 2 * NB
    slot_rows = ORB * CAP
    core_values = core_hamiltonian(key).reshape(devices, ROWS, M)
    halo_cols = core_values[:, :, ROWS:].reshape(devices, ROWS, blocks, slot_rows)
    halo_cols = jnp.transpose(halo_cols, (0, 2, 3, 1))
    sender_ids = jnp.arange(devices, dtype=jnp.int32)[:, None]
    block_ids = jnp.arange(blocks, dtype=jnp.int32)[None, :]
    holder_ids = ((sender_ids - neighbour_offsets_drawn()[None, :]) % devices).astype(jnp.int32)
    mirrored = halo_cols[holder_ids, block_ids]
    block_shape = (devices, blocks, slot_rows, M - ROWS)
    base_key = jax.random.fold_in(key, 23)
    fresh_part = coupling(jax.random.fold_in(base_key, 1), block_shape)
    block_iota = lax.broadcasted_iota(jnp.int32, block_shape, 1)
    row_ids = lax.broadcasted_iota(jnp.int32, block_shape, 2)
    col_ids = lax.broadcasted_iota(jnp.int32, block_shape, 3)
    levels = onsite_values(jax.random.fold_in(base_key, 2), row_ids[:, :, :, :1])
    fresh_part = jnp.where(col_ids == block_iota * slot_rows + row_ids, levels, fresh_part)
    return jnp.concatenate([mirrored, fresh_part], axis=3)


def draw_halo_request(key, part):
    devices = NORB // ROWS
    blocks = 2 * NB
    base_key = jax.random.fold_in(key, 37)
    hot_owner = jax.random.randint(jax.random.fold_in(base_key, 1), (), 0, devices)
    heavy_rows = jax.random.randint(jax.random.fold_in(base_key, 2), (devices, 1), 0, 4) == 0
    counts = jax.random.randint(jax.random.fold_in(base_key, 3), (devices, blocks), 0, CAP + 1)
    requester = lax.broadcasted_iota(jnp.int32, (devices, blocks), 0)
    owner_ids = (requester + neighbour_offsets_drawn()[None, :]) % devices
    full = heavy_rows | (owner_ids == hot_owner) | (requester == hot_owner)
    counts = jnp.where(full, CAP, counts)
    starts = jax.random.randint(jax.random.fold_in(base_key, 4), (devices, blocks, 1), 0, ATOM_DEV)
    slot_ids = lax.broadcasted_iota(jnp.int32, (devices, blocks, CAP), 2)
    atom_ids = (starts + slot_ids * (ATOM_DEV // CAP)) % ATOM_DEV
    chosen = jnp.where(slot_ids < counts[:, :, None], atom_ids, -1)
    return chosen.reshape(devices, blocks * CAP).astype(jnp.int32)


def set_ends(result, own_key, least, high):
    shape = result.shape
    index_at = [jax.random.randint(jax.random.fold_in(own_key, axis), (), 0, shape[axis]) for axis in range(len(shape))]
    result = result.at[tuple(index_at)].set(least)
    longest = shape.index(max(shape))
    index_at[longest] = (index_at[longest] + 1) % shape[longest]
    return result.at[tuple(index_at)].set(high)


def steps_of(stream_key, dims, cuts, least, high):
    def one(position, parts):
        steps = jax.random.uniform(jax.random.fold_in(jax.random.fold_in(stream_key, 6), position), (parts,), jnp.float32, least / len(cuts), high / len(cuts))
        return jnp.repeat(jnp.exp(steps), dims[position] // parts).reshape((-1,) + (1,) * (len(dims) - position - 1))

    loudness = one(*cuts[0])
    for cut in cuts[1:]:
        loudness = loudness * one(*cut)
    return loudness


def normal_values(own_key, shape, width, limit, cuts=(), held_as=jnp.bfloat16):
    entries = jax.random.normal(own_key, shape, jnp.float32) * width
    if len(cuts) > 0:
        entries = steps_of(own_key, shape, cuts, -0.22, 0.18) * entries
    return jnp.clip(entries, min=-limit, max=limit).astype(held_as)


def setup_inputs(seed: int = 0) -> dict:
    seeds = jax.random.split(jax.random.key(seed), 8)
    ham_core = draw_ham_core(jax.random.fold_in(seeds[7], 71), 0)
    halo_rows = draw_halo_rows(jax.random.fold_in(seeds[7], 71), 0)
    halo_request = draw_halo_request(jax.random.fold_in(seeds[7], 71), 0)
    deriv = normal_values(seeds[3], (3, ATOMS, ORB, M), 2.5, 15.0, ((1, 128),), jnp.float32)
    e_low = jnp.clip(jax.random.uniform(seeds[4], (1,), jnp.float32, -8.0, -5.0), -8.0, -5.0)
    e_high = jnp.clip(jax.random.uniform(seeds[5], (1,), jnp.float32, 4.5, 7.5), 4.5, 7.5)
    branches = set_ends(jax.random.randint(seeds[6], (ITERS,), 0, 2), jax.random.fold_in(seeds[6], 1), 0, 1).astype(jnp.int32)
    return {"ham_core": ham_core, "halo_rows": halo_rows, "halo_request": halo_request, "deriv": deriv, "e_low": e_low, "e_high": e_high, "branches": branches}


def product(left, right):
    return jnp.dot(left, right, precision=lax.Precision.HIGHEST, preferred_element_type=jnp.float32)


def neighbour_offsets():
    blocks = jnp.arange(2 * NB, dtype=jnp.int32)
    return jnp.where(blocks < NB, blocks + 1, NB - 1 - blocks).astype(jnp.int32)


def partition(part_index, ham_core, halo_rows, halo_request, deriv, e_low, e_high, branches):
    core_rows = lax.dynamic_slice_in_dim(ham_core, part_index * ROWS, ROWS, 0)
    owners = ((part_index + neighbour_offsets()) % N_DOM).astype(jnp.int32)
    halo_block = halo_rows[owners, jnp.arange(2 * NB, dtype=jnp.int32)]
    halo_block = halo_block.reshape(ORB * HALO_SLOTS, M)
    request = lax.dynamic_index_in_dim(halo_request, part_index, 0, keepdims=False)
    live_halo = jnp.repeat((request >= 0).astype(jnp.float32), ORB)
    live_mask = jnp.concatenate([jnp.ones((ROWS,), jnp.float32), live_halo])
    whole_ham = jnp.concatenate([core_rows, halo_block], axis=0) * live_mask[:, None] * live_mask[None, :]
    symmetric = 0.5 * (whole_ham + whole_ham.T)
    spread = e_high[0] - e_low[0]
    projector = (jnp.diag(e_high[0] * live_mask) - symmetric) / spread
    for number in range(ITERS):
        square = product(projector, projector)
        projector = jnp.where(branches[number] == 1, 2.0 * projector - square, square)
    core_density = projector[:ROWS]
    blocks = lax.dynamic_slice_in_dim(deriv, part_index * ATOM_DEV, ATOM_DEV, 1)
    weighted = jnp.sum(core_density.reshape(ATOM_DEV, ORB, M)[None] * blocks, axis=2)
    pair_force = 2.0 * jnp.sum(weighted.reshape(3, ATOM_DEV, ATOM_S, ORB), axis=3)
    own_force = jnp.sum(pair_force, axis=2)
    reaction = -jnp.sum(pair_force, axis=1)
    core_ids = part_index * ATOM_DEV + jnp.arange(ATOM_DEV, dtype=jnp.int32)
    slot_owner = jnp.repeat(owners, CAP).astype(jnp.int32)
    halo_ids = jnp.where(request >= 0, slot_owner * ATOM_DEV + request, ATOMS).astype(jnp.int32)
    all_ids = jnp.concatenate([core_ids, halo_ids])
    return core_density, own_force, reaction, core_ids, all_ids


def reference(ham_core, halo_rows, halo_request, deriv, e_low, e_high, branches):
    def visit(totals, part_index):
        core_density, own_force, reaction, core_ids, all_ids = partition(part_index, ham_core, halo_rows, halo_request, deriv, e_low, e_high, branches)
        totals = totals.at[:, all_ids].add(reaction, mode="drop")
        totals = totals.at[:, core_ids].add(own_force)
        return totals, core_density

    forces, stacked = lax.scan(visit, jnp.zeros((3, ATOMS), jnp.float32), jnp.arange(N_DOM, dtype=jnp.int32))
    return stacked.reshape(NORB, M), forces
```

```python
import jax
import jax.numpy as jnp
from jax import lax
from jax.experimental import pallas as pl
from jax.experimental.pallas import tpu as pltpu
from jax.sharding import PartitionSpec as P

ORB = 4
ATOM_DEV = 160
NB = 4
BLOCKS = 2 * NB
ITERS = 5
ROWS = 640
M = 1280
SLOT_ROWS = ROWS // BLOCKS
TILE = 256
COLS = M // TILE
F32 = jnp.float32
BF16 = jnp.bfloat16
MESH = pl.DeviceIdType.MESH


def block_offset(block):
    if block < NB:
        return block + 1
    return NB - 1 - block


def mm(left, right):
    return jnp.dot(left, right, preferred_element_type=F32)


def mm_nt(left, right):
    return lax.dot_general(left, right, (((1,), (1,)), ((), ())), preferred_element_type=F32)


def span(i):
    return slice(i * TILE, (i + 1) * TILE)


def split2(value):
    high = value.astype(BF16)
    return high, (value - high.astype(F32)).astype(BF16)


def split3(value):
    high = value.astype(BF16)
    rest = value - high.astype(F32)
    mid = rest.astype(BF16)
    return high, mid, (rest - mid.astype(F32)).astype(BF16)


def sp2_kernel(
    low_ref, high_ref, branch_ref, request_ref, ham_ref, halo_ref, deriv_ref,
    dens_ref, force_ref,
    core, halo, dbuf, xh, xl, acc, dens, own, select, rsum, fsend, frecv,
    core_sem, deriv_sem, dens_sem, send_sem, recv_sem, fsend_sem, frecv_sem,
):
    count = lax.axis_size("dom")
    me = lax.axis_index("dom")

    def peer(offset):
        return lax.rem(me + offset + count, count)

    load_core = pltpu.make_async_copy(ham_ref, core, core_sem.at[0])
    load_core.start()
    barrier = pltpu.get_barrier_semaphore()
    for k in range(BLOCKS):
        pl.semaphore_signal(barrier, inc=1, device_id=(peer(block_offset(k)),), device_id_type=MESH)
    pl.semaphore_wait(barrier, BLOCKS)
    sends = []
    for k in (3, 7, 2, 6, 1, 5, 0, 4):
        send = pltpu.make_async_remote_copy(
            src_ref=halo_ref.at[0, k, :, ROWS:M],
            dst_ref=halo.at[k * SLOT_ROWS : (k + 1) * SLOT_ROWS],
            send_sem=send_sem.at[k],
            recv_sem=recv_sem.at[k],
            device_id=(peer(-block_offset(k)),),
            device_id_type=MESH,
        )
        send.start()
        sends.append(send)
    load_deriv = []
    for c in range(3):
        for mu in range(ORB):
            load = pltpu.make_async_copy(deriv_ref.at[c, :, mu, :], dbuf.at[c, mu], deriv_sem.at[c * ORB + mu])
            load.start()
            load_deriv.append(load)

    request = request_ref[...]
    live = (request >= 0).astype(F32)
    spread_atom = (
        lax.broadcasted_iota(jnp.int32, (ROWS, ATOM_DEV), 0) // ORB
        == lax.broadcasted_iota(jnp.int32, (ROWS, ATOM_DEV), 1)
    ).astype(F32)
    live_col = jnp.sum(spread_atom * live, axis=1, keepdims=True)
    eight = jnp.broadcast_to(live, (8, ATOM_DEV))
    live_row = mm_nt(eight.astype(BF16), spread_atom.astype(BF16))[0:1]
    ids = jnp.broadcast_to(request.astype(F32), (8, ATOM_DEV))
    slot_atom = mm_nt(ids.astype(BF16), spread_atom.astype(BF16))[0:1]
    lane_block = lax.broadcasted_iota(jnp.int32, (1, ROWS), 1) // SLOT_ROWS
    atom_row = lax.broadcasted_iota(jnp.int32, (ATOM_DEV, ROWS), 0).astype(F32)
    for k in range(BLOCKS):
        wanted = jnp.where(lane_block == k, slot_atom, -1.0)
        select[k] = (atom_row == wanted).astype(BF16)
    fsend[...] = jnp.zeros_like(fsend)
    rsum[...] = jnp.zeros_like(rsum)
    own[...] = jnp.zeros_like(own)

    high = high_ref[0]
    inverse = 1.0 / jnp.broadcast_to(high - low_ref[0], (1, ROWS))
    diagonal = (
        lax.broadcasted_iota(jnp.int32, (ROWS, ROWS), 0)
        == lax.broadcasted_iota(jnp.int32, (ROWS, ROWS), 1)
    ).astype(F32) * high

    def step(i):
        taken = branch_ref[i].astype(F32)
        return 2.0 * taken, 1.0 - 2.0 * taken

    def square_block(src, rows, cols, depth):
        lh = xh[src, rows, depth]
        ll = xl[src, rows, depth]
        rh = xh[src, depth, cols]
        rl = xl[src, depth, cols]
        return mm(lh, rh) + mm(ll, rh) + mm(lh, rl)

    def finish(src, dst, i, j, square, scale):
        old = xh[src, span(i), span(j)].astype(F32) + xl[src, span(i), span(j)].astype(F32)
        new = scale[0] * old + scale[1] * square
        h, l = split2(new)
        xh[dst, span(i), span(j)] = h
        xl[dst, span(i), span(j)] = l
        if i < j:
            th, tl = split2(new.T)
            xh[dst, span(j), span(i)] = th
            xl[dst, span(j), span(i)] = tl

    load_core.wait()
    own_part = core[:, 0:ROWS]
    start = (diagonal - 0.5 * (own_part + own_part.T)) * inverse
    h, l = split2(start)
    xh[0, 0:ROWS, 0:ROWS] = h
    xl[0, 0:ROWS, 0:ROWS] = l
    cross = -(core[:, ROWS:M] * live_row) * inverse
    h, l = split2(cross)
    xh[0, 0:ROWS, ROWS:M] = h
    xl[0, 0:ROWS, ROWS:M] = l
    h, l = split2(cross.T)
    xh[0, ROWS:M, 0:ROWS] = h
    xl[0, ROWS:M, 0:ROWS] = l
    scale = step(0)
    for j in range(COLS):
        for i in range(j + 1):
            if j < 2:
                finish(0, 1, i, j, square_block(0, span(i), span(j), slice(0, M)), scale)
            elif i < 2:
                acc[span(i), span(j)] = square_block(0, span(i), span(j), slice(0, ROWS))

    for send in sends:
        send.wait()
    received = halo[...]
    start = (diagonal * live_col - 0.5 * (received + received.T) * live_col * live_row) * inverse
    h, l = split2(start)
    xh[0, ROWS:M, ROWS:M] = h
    xl[0, ROWS:M, ROWS:M] = l
    for j in range(2, COLS):
        for i in range(j + 1):
            if i < 2:
                part = acc[span(i), span(j)] + square_block(0, span(i), span(j), slice(ROWS, M))
            else:
                part = square_block(0, span(i), span(j), slice(0, M))
            finish(0, 1, i, j, part, scale)

    def middle(number, carry):
        src = lax.rem(number, 2)
        dst = 1 - src
        weights = step(number)
        for j in range(COLS):
            for i in range(j + 1):
                finish(src, dst, i, j, square_block(src, span(i), span(j), slice(0, M)), weights)
        return carry

    lax.fori_loop(1, ITERS - 1, middle, 0)

    last = (ITERS - 1) % 2
    scale = step(ITERS - 1)
    for load in load_deriv:
        load.wait()
    zero = jnp.zeros((8, 128), F32)
    writes = []

    def column(q):
        old = xh[last, 0:ROWS, span(q)].astype(F32) + xl[last, 0:ROWS, span(q)].astype(F32)
        square = square_block(last, slice(0, ROWS), span(q), slice(0, M))
        new = scale[0] * old + scale[1] * square
        for side in range(2):
            tile = 2 * q + side
            lanes = slice(tile * 128, (tile + 1) * 128)
            dens[tile] = new[:, side * 128 : (side + 1) * 128]
            write = pltpu.make_async_copy(dens.at[tile], dens_ref.at[:, lanes], dens_sem.at[tile])
            write.start()
            writes.append(write)

        def group(g, sums):
            sums = [list(pair) for pair in sums]
            atoms = pl.ds(pl.multiple_of(g * 8, 8), 8)
            local = [None, None, None]
            for side in range(2):
                lanes = slice(q * TILE + side * 128, q * TILE + (side + 1) * 128)
                rows = [dens[2 * q + side, pl.ds(g * 8 * ORB + mu, 8, stride=ORB)] for mu in range(ORB)]
                for c in range(3):
                    term = rows[0] * dbuf[c, 0, atoms, lanes]
                    for mu in range(1, ORB):
                        term = term + rows[mu] * dbuf[c, mu, atoms, lanes]
                    sums[c][side] = sums[c][side] + term
                    local[c] = term if side == 0 else local[c] + term
            for c in range(3):
                own[c, atoms] += local[c]
            return tuple(tuple(pair) for pair in sums)

        sums = lax.fori_loop(0, ATOM_DEV // 8, group, ((zero, zero),) * 3, unroll=4)
        return [[jnp.sum(value, axis=0, keepdims=True) for value in pair] for pair in sums]

    def by_parts(sums):
        for c in range(3):
            rsum[c : c + 1] = jnp.concatenate([piece[c] for piece in sums], axis=1)
        parts = split3(rsum[0:8])
        return jnp.concatenate([p.astype(F32) for p in parts], axis=0).astype(BF16)

    def joined(value):
        return value[0:8] + value[8:16] + value[16:24]

    def halves(triples, which):
        return [t[which] for t in triples]

    two = column(2)
    three = column(3)
    four = column(4)
    halo_sums = by_parts([halves(two, 1), halves(three, 0), halves(three, 1), halves(four, 0), halves(four, 1)])
    exchanges = []
    for k in range(BLOCKS):
        terms = -2.0 * joined(mm_nt(halo_sums, select[k]))
        fsend[k, :, 0:ATOM_DEV] = terms
        send = pltpu.make_async_remote_copy(
            src_ref=fsend.at[k],
            dst_ref=frecv.at[k],
            send_sem=fsend_sem.at[k],
            recv_sem=frecv_sem.at[k],
            device_id=(peer(block_offset(k)),),
            device_id_type=MESH,
        )
        send.start()
        exchanges.append(send)
    zeroth = column(0)
    first = column(1)
    core_sums = by_parts([halves(zeroth, 0), halves(zeroth, 1), halves(first, 0), halves(first, 1), halves(two, 0)])
    atom_of_lane = (
        lax.broadcasted_iota(jnp.int32, (ATOM_DEV, ROWS), 1) // ORB
        == lax.broadcasted_iota(jnp.int32, (ATOM_DEV, ROWS), 0)
    ).astype(BF16)
    total = -2.0 * joined(mm_nt(core_sums, atom_of_lane))
    ones = jnp.ones((8, 3 * 128), BF16)
    row_of = lax.broadcasted_iota(jnp.int32, (8, ATOM_DEV), 0)
    for c in range(3):
        parts = jnp.concatenate([p.astype(F32) for p in split3(own[c])], axis=1).astype(BF16)
        total = total + jnp.where(row_of == c, 2.0 * mm_nt(ones, parts), 0.0)
    for exchange in exchanges:
        exchange.wait()
    for k in range(BLOCKS):
        total = total + frecv[k, :, 0:ATOM_DEV]
    force_ref[...] = total[0:3]
    for write in writes:
        write.wait()


def per_device(ham_core, halo_rows, halo_request, deriv, e_low, e_high, branches):
    smem = pl.BlockSpec(memory_space=pltpu.SMEM)
    vmem = pl.BlockSpec(memory_space=pltpu.VMEM)
    hbm = pl.BlockSpec(memory_space=pl.ANY)
    dma = pltpu.SemaphoreType.DMA
    return pl.pallas_call(
        sp2_kernel,
        out_shape=(
            jax.ShapeDtypeStruct((ROWS, M), F32),
            jax.ShapeDtypeStruct((3, ATOM_DEV), F32),
        ),
        in_specs=[smem, smem, smem, vmem, hbm, hbm, hbm],
        out_specs=(hbm, vmem),
        scratch_shapes=[
            pltpu.VMEM((ROWS, M), F32),
            pltpu.VMEM((ROWS, ROWS), F32),
            pltpu.VMEM((3, ORB, ATOM_DEV, M), F32),
            pltpu.VMEM((2, M, M), BF16),
            pltpu.VMEM((2, M, M), BF16),
            pltpu.VMEM((2 * TILE, M), F32),
            pltpu.VMEM((2 * COLS, ROWS, 128), F32),
            pltpu.VMEM((3, ATOM_DEV, 128), F32),
            pltpu.VMEM((BLOCKS, ATOM_DEV, ROWS), BF16),
            pltpu.VMEM((8, ROWS), F32),
            pltpu.VMEM((BLOCKS, 8, TILE), F32),
            pltpu.VMEM((BLOCKS, 8, TILE), F32),
            dma((1,)),
            dma((3 * ORB,)),
            dma((2 * COLS,)),
            dma((BLOCKS,)),
            dma((BLOCKS,)),
            dma((BLOCKS,)),
            dma((BLOCKS,)),
        ],
        compiler_params=pltpu.CompilerParams(
            collective_id=0, has_side_effects=True, vmem_limit_bytes=60 << 20
        ),
    )(e_low, e_high, branches, halo_request, ham_core, halo_rows, deriv)


def solution(mesh):
    in_specs = (
        P("dom", None),
        P("dom", None, None, None),
        P("dom", None),
        P(None, "dom", None, None),
        P(),
        P(),
        P(),
    )
    out_specs = (P("dom", None), P(None, "dom"))
    return jax.shard_map(
        per_device, mesh=mesh, in_specs=in_specs, out_specs=out_specs, check_vma=False
    )
```

```python
import jax
import jax.numpy as jnp
from jax import lax
from jax.experimental import pallas as pl
from jax.experimental.pallas import tpu as pltpu
from jax.sharding import PartitionSpec as P

ORB = 4
ATOM_DEV = 160
NB = 4
BLOCKS = 2 * NB
ITERS = 5
ROWS = 640
M = 1280
SLOT_ROWS = ROWS // BLOCKS
TILE = 256
COLS = M // TILE
F32 = jnp.float32
BF16 = jnp.bfloat16
MESH = pl.DeviceIdType.MESH


def block_offset(block):
    if block < NB:
        return block + 1
    return NB - 1 - block


def mm(left, right):
    return jnp.dot(left, right, preferred_element_type=F32)


def mm_nt(left, right):
    return lax.dot_general(left, right, (((1,), (1,)), ((), ())), preferred_element_type=F32)


def span(i):
    return slice(i * TILE, (i + 1) * TILE)


def split2(value):
    high = value.astype(BF16)
    return high, (value - high.astype(F32)).astype(BF16)


def split3(value):
    high = value.astype(BF16)
    rest = value - high.astype(F32)
    mid = rest.astype(BF16)
    return high, mid, (rest - mid.astype(F32)).astype(BF16)


def sp2_kernel(
    low_ref, high_ref, branch_ref, request_ref, ham_ref, halo_ref, deriv_ref,
    dens_ref, force_ref,
    core, halo, dbuf, even_h, even_l, odd_h, odd_l, acc, dens, own, select, rsum, fsend, frecv,
    core_sem, deriv_sem, send_sem, recv_sem, fsend_sem, frecv_sem,
):
    count = lax.axis_size("dom")
    me = lax.axis_index("dom")

    def peer(offset):
        return lax.rem(me + offset + count, count)

    load_core = pltpu.make_async_copy(ham_ref, core, core_sem.at[0])
    load_core.start()
    barrier = pltpu.get_barrier_semaphore()
    for k in range(BLOCKS):
        pl.semaphore_signal(barrier, inc=1, device_id=(peer(block_offset(k)),), device_id_type=MESH)
    pl.semaphore_wait(barrier, BLOCKS)
    sends = []
    for k in (3, 7, 2, 6, 1, 5, 0, 4):
        send = pltpu.make_async_remote_copy(
            src_ref=halo_ref.at[0, k, :, ROWS:M],
            dst_ref=halo.at[k * SLOT_ROWS : (k + 1) * SLOT_ROWS],
            send_sem=send_sem.at[k],
            recv_sem=recv_sem.at[k],
            device_id=(peer(-block_offset(k)),),
            device_id_type=MESH,
        )
        send.start()
        sends.append(send)
    load_deriv = []
    for c in range(3):
        for mu in range(ORB):
            load = pltpu.make_async_copy(deriv_ref.at[c, :, mu, :], dbuf.at[c, mu], deriv_sem.at[c * ORB + mu])
            load.start()
            load_deriv.append(load)

    request = request_ref[...]
    live = (request >= 0).astype(F32)
    spread_atom = (
        lax.broadcasted_iota(jnp.int32, (ROWS, ATOM_DEV), 0) // ORB
        == lax.broadcasted_iota(jnp.int32, (ROWS, ATOM_DEV), 1)
    ).astype(F32)
    live_col = jnp.sum(spread_atom * live, axis=1, keepdims=True)
    eight = jnp.broadcast_to(live, (8, ATOM_DEV))
    live_row = mm_nt(eight.astype(BF16), spread_atom.astype(BF16))[0:1]
    ids = jnp.broadcast_to(request.astype(F32), (8, ATOM_DEV))
    slot_atom = mm_nt(ids.astype(BF16), spread_atom.astype(BF16))[0:1]
    lane_block = lax.broadcasted_iota(jnp.int32, (1, ROWS), 1) // SLOT_ROWS
    atom_row = lax.broadcasted_iota(jnp.int32, (ATOM_DEV, ROWS), 0).astype(F32)
    for k in range(BLOCKS):
        wanted = jnp.where(lane_block == k, slot_atom, -1.0)
        select[k] = (atom_row == wanted).astype(BF16)
    fsend[...] = jnp.zeros_like(fsend)
    rsum[...] = jnp.zeros_like(rsum)
    own[...] = jnp.zeros_like(own)

    high = high_ref[0]
    inverse = 1.0 / jnp.broadcast_to(high - low_ref[0], (1, ROWS))
    diagonal = (
        lax.broadcasted_iota(jnp.int32, (ROWS, ROWS), 0)
        == lax.broadcasted_iota(jnp.int32, (ROWS, ROWS), 1)
    ).astype(F32) * high

    def step(i):
        taken = branch_ref[i].astype(F32)
        return 2.0 * taken, 1.0 - 2.0 * taken

    pairs = ((even_h, even_l), (odd_h, odd_l))
    first_h, first_l = pairs[0]

    def square_block(src, rows, cols, depth):
        xh, xl = pairs[src]
        rh = xh[depth, cols]
        return mm(xh[rows, depth], rh) + mm(xl[rows, depth], rh) + mm(xh[rows, depth], xl[depth, cols])

    def finish(src, dst, i, j, square, scale):
        xh, xl = pairs[src]
        yh, yl = pairs[dst]
        old = xh[span(i), span(j)].astype(F32) + xl[span(i), span(j)].astype(F32)
        new = scale[0] * old + scale[1] * square
        yh[span(i), span(j)], yl[span(i), span(j)] = split2(new)
        if i < j:
            yh[span(j), span(i)], yl[span(j), span(i)] = split2(new.T)

    load_core.wait()
    own_part = core[:, 0:ROWS]
    start = (diagonal - 0.5 * (own_part + own_part.T)) * inverse
    h, l = split2(start)
    first_h[0:ROWS, 0:ROWS] = h
    first_l[0:ROWS, 0:ROWS] = l
    cross = -(core[:, ROWS:M] * live_row) * inverse
    h, l = split2(cross)
    first_h[0:ROWS, ROWS:M] = h
    first_l[0:ROWS, ROWS:M] = l
    h, l = split2(cross.T)
    first_h[ROWS:M, 0:ROWS] = h
    first_l[ROWS:M, 0:ROWS] = l
    scale = step(0)
    for j in range(COLS):
        for i in range(j + 1):
            if j < 2:
                finish(0, 1, i, j, square_block(0, span(i), span(j), slice(0, M)), scale)
            elif i < 2:
                acc[span(i), span(j)] = square_block(0, span(i), span(j), slice(0, ROWS))

    for send in sends:
        send.wait()
    received = halo[...]
    start = (diagonal * live_col - 0.5 * (received + received.T) * live_col * live_row) * inverse
    h, l = split2(start)
    first_h[ROWS:M, ROWS:M] = h
    first_l[ROWS:M, ROWS:M] = l
    for j in range(2, COLS):
        for i in range(j + 1):
            if i < 2:
                part = acc[span(i), span(j)] + square_block(0, span(i), span(j), slice(ROWS, M))
            else:
                part = square_block(0, span(i), span(j), slice(0, M))
            finish(0, 1, i, j, part, scale)

    for number in range(1, ITERS - 1):
        src = number % 2
        weights = step(number)
        for j in range(COLS):
            for i in range(j + 1):
                finish(src, 1 - src, i, j, square_block(src, span(i), span(j), slice(0, M)), weights)

    last = (ITERS - 1) % 2
    scale = step(ITERS - 1)
    for load in load_deriv:
        load.wait()
    zero = jnp.zeros((8, 128), F32)

    def column(q):
        xh, xl = pairs[last]
        old = xh[0:ROWS, span(q)].astype(F32) + xl[0:ROWS, span(q)].astype(F32)
        square = square_block(last, slice(0, ROWS), span(q), slice(0, M))
        new = scale[0] * old + scale[1] * square
        for side in range(2):
            tile = 2 * q + side
            dens[tile] = new[:, side * 128 : (side + 1) * 128]
        dens_ref[:, span(q)] = new

        def group(g, sums):
            sums = [list(pair) for pair in sums]
            atoms = slice(g * 8, g * 8 + 8)
            local = [None, None, None]
            for side in range(2):
                lanes = slice(q * TILE + side * 128, q * TILE + (side + 1) * 128)
                rows = [dens[2 * q + side, pl.ds(g * 8 * ORB + mu, 8, stride=ORB)] for mu in range(ORB)]
                for c in range(3):
                    term = rows[0] * dbuf[c, 0, atoms, lanes]
                    for mu in range(1, ORB):
                        term = term + rows[mu] * dbuf[c, mu, atoms, lanes]
                    sums[c][side] = sums[c][side] + term
                    local[c] = term if side == 0 else local[c] + term
            for c in range(3):
                own[c, atoms] += local[c]
            return tuple(tuple(pair) for pair in sums)

        sums = ((zero, zero),) * 3
        for g in range(ATOM_DEV // 8):
            sums = group(g, sums)
        return [[jnp.sum(value, axis=0, keepdims=True) for value in pair] for pair in sums]

    def by_parts(sums):
        for c in range(3):
            rsum[c : c + 1] = jnp.concatenate([piece[c] for piece in sums], axis=1)
        parts = split3(rsum[0:8])
        return jnp.concatenate([p.astype(F32) for p in parts], axis=0).astype(BF16)

    def joined(value):
        return value[0:8] + value[8:16] + value[16:24]

    def halves(triples, which):
        return [t[which] for t in triples]

    two = column(2)
    three = column(3)
    four = column(4)
    halo_sums = by_parts([halves(two, 1), halves(three, 0), halves(three, 1), halves(four, 0), halves(four, 1)])
    exchanges = []
    for k in range(BLOCKS):
        terms = -2.0 * joined(mm_nt(halo_sums, select[k]))
        fsend[k, :, 0:ATOM_DEV] = terms
        send = pltpu.make_async_remote_copy(
            src_ref=fsend.at[k],
            dst_ref=frecv.at[k],
            send_sem=fsend_sem.at[k],
            recv_sem=frecv_sem.at[k],
            device_id=(peer(block_offset(k)),),
            device_id_type=MESH,
        )
        send.start()
        exchanges.append(send)
    zeroth = column(0)
    first = column(1)
    core_sums = by_parts([halves(zeroth, 0), halves(zeroth, 1), halves(first, 0), halves(first, 1), halves(two, 0)])
    atom_of_lane = (
        lax.broadcasted_iota(jnp.int32, (ATOM_DEV, ROWS), 1) // ORB
        == lax.broadcasted_iota(jnp.int32, (ATOM_DEV, ROWS), 0)
    ).astype(BF16)
    total = -2.0 * joined(mm_nt(core_sums, atom_of_lane))
    ones = jnp.ones((8, 3 * 128), BF16)
    row_of = lax.broadcasted_iota(jnp.int32, (8, ATOM_DEV), 0)
    for c in range(3):
        parts = jnp.concatenate([p.astype(F32) for p in split3(own[c])], axis=1).astype(BF16)
        total = total + jnp.where(row_of == c, 2.0 * mm_nt(ones, parts), 0.0)
    for exchange in exchanges:
        exchange.wait()
    for k in range(BLOCKS):
        total = total + frecv[k, :, 0:ATOM_DEV]
    force_ref[...] = total[0:3]


def per_device(ham_core, halo_rows, halo_request, deriv, e_low, e_high, branches):
    smem = pl.BlockSpec(memory_space=pltpu.SMEM)
    vmem = pl.BlockSpec(memory_space=pltpu.VMEM)
    hbm = pl.BlockSpec(memory_space=pl.ANY)
    dma = pltpu.SemaphoreType.DMA
    return pl.pallas_call(
        sp2_kernel,
        out_shape=(
            pltpu.VMEM((ROWS, M), F32),
            pltpu.VMEM((3, ATOM_DEV), F32),
        ),
        in_specs=[smem, smem, smem, vmem, hbm, hbm, hbm],
        out_specs=(vmem, vmem),
        scratch_shapes=[
            pltpu.VMEM((ROWS, M), F32),
            pltpu.VMEM((ROWS, ROWS), F32),
            pltpu.VMEM((3, ORB, ATOM_DEV, M), F32),
            pltpu.VMEM((M, M), BF16),
            pltpu.VMEM((M, M), BF16),
            pltpu.VMEM((M, M), BF16),
            pltpu.VMEM((M, M), BF16),
            pltpu.VMEM((2 * TILE, M), F32),
            pltpu.VMEM((2 * COLS, ROWS, 128), F32),
            pltpu.VMEM((3, ATOM_DEV, 128), F32),
            pltpu.VMEM((BLOCKS, ATOM_DEV, ROWS), BF16),
            pltpu.VMEM((8, ROWS), F32),
            pltpu.VMEM((BLOCKS, 8, TILE), F32),
            pltpu.VMEM((BLOCKS, 8, TILE), F32),
            dma((1,)),
            dma((3 * ORB,)),
            dma((BLOCKS,)),
            dma((BLOCKS,)),
            dma((BLOCKS,)),
            dma((BLOCKS,)),
        ],
        compiler_params=pltpu.CompilerParams(
            collective_id=0, has_side_effects=True, vmem_limit_bytes=52 << 20
        ),
    )(e_low, e_high, branches, halo_request, ham_core, halo_rows, deriv)


def solution(mesh):
    in_specs = (
        P("dom", None),
        P("dom", None, None, None),
        P("dom", None),
        P(None, "dom", None, None),
        P(),
        P(),
        P(),
    )
    out_specs = (P("dom", None), P(None, "dom"))
    return jax.shard_map(
        per_device, mesh=mesh, in_specs=in_specs, out_specs=out_specs, check_vma=False
    )
```

```python
import jax
import jax.numpy as jnp
from jax import lax
from jax.experimental import pallas as pl
from jax.experimental.pallas import tpu as pltpu
from jax.sharding import PartitionSpec as P

ORB = 4
ATOM_DEV = 160
NB = 4
BLOCKS = 2 * NB
ITERS = 5
ROWS = 640
M = 1280
SLOT_ROWS = ROWS // BLOCKS
TILE = 256
COLS = M // TILE
F32 = jnp.float32
BF16 = jnp.bfloat16
CUTS = (0, 384, 640)
MESH = pl.DeviceIdType.MESH


def block_offset(block):
    if block < NB:
        return block + 1
    return NB - 1 - block


def mm(left, right):
    return jnp.dot(left, right, preferred_element_type=F32)


def mm_nt(left, right):
    return lax.dot_general(left, right, (((1,), (1,)), ((), ())), preferred_element_type=F32)


def span(i):
    return slice(i * TILE, (i + 1) * TILE)


def split2(value):
    high = value.astype(BF16)
    return high, (value - high.astype(F32)).astype(BF16)


def split3(value):
    high = value.astype(BF16)
    rest = value - high.astype(F32)
    mid = rest.astype(BF16)
    return high, mid, (rest - mid.astype(F32)).astype(BF16)


def sp2_kernel(
    low_ref, high_ref, branch_ref, request_ref, ham_ref, halo_ref, deriv_ref,
    dens_ref, force_ref,
    core, halo, dbuf, even_h, even_l, odd_h, odd_l, acc, dens, own, select, rsum, fsend, frecv,
    core_sem, deriv_sem, send_sem, recv_sem, fsend_sem, frecv_sem,
):
    count = lax.axis_size("dom")
    me = lax.axis_index("dom")

    def peer(offset):
        return lax.rem(me + offset + count, count)

    load_core = pltpu.make_async_copy(ham_ref, core, core_sem.at[0])
    load_core.start()
    barrier = pltpu.get_barrier_semaphore()
    for k in range(BLOCKS):
        pl.semaphore_signal(barrier, inc=1, device_id=(peer(block_offset(k)),), device_id_type=MESH)
    pl.semaphore_wait(barrier, BLOCKS)

    def halo_copy(phase, k):
        return pltpu.make_async_remote_copy(
            src_ref=halo_ref.at[0, k, :, ROWS + CUTS[phase] : ROWS + CUTS[phase + 1]],
            dst_ref=halo.at[k * SLOT_ROWS : (k + 1) * SLOT_ROWS, CUTS[phase] : CUTS[phase + 1]],
            send_sem=send_sem.at[phase, k],
            recv_sem=recv_sem.at[phase, k],
            device_id=(peer(-block_offset(k)),),
            device_id_type=MESH,
        )

    def send_all(order):
        for phase in range(2):
            for k in order:
                halo_copy(phase, k).start()

    on_first = lax.rem(me, 2) == 0
    pl.when(on_first)(lambda: send_all((3, 7, 2, 6, 1, 5, 0, 4)))
    pl.when(jnp.logical_not(on_first))(lambda: send_all((0, 4, 1, 5, 2, 6, 3, 7)))
    load_deriv = []
    for c in range(3):
        for mu in range(ORB):
            load = pltpu.make_async_copy(deriv_ref.at[c, :, mu, :], dbuf.at[c, mu], deriv_sem.at[c * ORB + mu])
            load.start()
            load_deriv.append(load)

    request = request_ref[...]
    live = (request >= 0).astype(F32)
    spread_atom = (
        lax.broadcasted_iota(jnp.int32, (ROWS, ATOM_DEV), 0) // ORB
        == lax.broadcasted_iota(jnp.int32, (ROWS, ATOM_DEV), 1)
    ).astype(F32)
    live_col = jnp.sum(spread_atom * live, axis=1, keepdims=True)
    eight = jnp.broadcast_to(live, (8, ATOM_DEV))
    live_row = mm_nt(eight.astype(BF16), spread_atom.astype(BF16))[0:1]
    ids = jnp.broadcast_to(request.astype(F32), (8, ATOM_DEV))
    slot_atom = mm_nt(ids.astype(BF16), spread_atom.astype(BF16))[0:1]
    lane_block = lax.broadcasted_iota(jnp.int32, (1, ROWS), 1) // SLOT_ROWS
    atom_row = lax.broadcasted_iota(jnp.int32, (ATOM_DEV, ROWS), 0).astype(F32)
    for k in range(BLOCKS):
        wanted = jnp.where(lane_block == k, slot_atom, -1.0)
        select[k] = (atom_row == wanted).astype(BF16)
    fsend[...] = jnp.zeros_like(fsend)
    rsum[...] = jnp.zeros_like(rsum)
    own[...] = jnp.zeros_like(own)

    high = high_ref[0]
    inverse = 1.0 / jnp.broadcast_to(high - low_ref[0], (1, ROWS))
    diagonal = (
        lax.broadcasted_iota(jnp.int32, (ROWS, ROWS), 0)
        == lax.broadcasted_iota(jnp.int32, (ROWS, ROWS), 1)
    ).astype(F32) * high

    def step(i):
        taken = branch_ref[i].astype(F32)
        return 2.0 * taken, 1.0 - 2.0 * taken

    pairs = ((even_h, even_l), (odd_h, odd_l))
    first_h, first_l = pairs[0]

    def square_block(src, rows, cols, depth):
        xh, xl = pairs[src]
        left = xh[rows, depth]
        right = xh[depth, cols]
        small = mm(left, xl[depth, cols])
        if rows == cols:
            return mm(left, right) + (small + small.T)
        return mm(left, right) + mm(xl[rows, depth], right) + small

    def finish(src, dst, i, j, square, scale):
        xh, xl = pairs[src]
        yh, yl = pairs[dst]
        old = xh[span(i), span(j)].astype(F32) + xl[span(i), span(j)].astype(F32)
        new = scale[0] * old + scale[1] * square
        yh[span(i), span(j)], yl[span(i), span(j)] = split2(new)
        if i < j:
            yh[span(j), span(i)], yl[span(j), span(i)] = split2(new.T)

    load_core.wait()
    own_part = core[:, 0:ROWS]
    start = (diagonal - 0.5 * (own_part + own_part.T)) * inverse
    h, l = split2(start)
    first_h[0:ROWS, 0:ROWS] = h
    first_l[0:ROWS, 0:ROWS] = l
    cross = -(core[:, ROWS:M] * live_row) * inverse
    h, l = split2(cross)
    first_h[0:ROWS, ROWS:M] = h
    first_l[0:ROWS, ROWS:M] = l
    h, l = split2(cross.T)
    first_h[ROWS:M, 0:ROWS] = h
    first_l[ROWS:M, 0:ROWS] = l
    scale = step(0)
    whole = slice(0, M)
    near = slice(ROWS, ROWS + CUTS[1])
    far = slice(ROWS + CUTS[1], M)
    later = [(i, j) for j in range(2, COLS) for i in range(j + 1)]

    def kept(i, j):
        return span(i), slice(j * TILE - 2 * TILE, (j + 1) * TILE - 2 * TILE)

    for i, j in ((0, 0), (0, 1), (1, 1)):
        finish(0, 1, i, j, square_block(0, span(i), span(j), whole), scale)
    for i, j in later:
        acc[kept(i, j)] = square_block(0, span(i), span(j), slice(0, ROWS))

    def halo_start(rows, cols):
        both = halo[rows, cols] + halo[cols, rows].T
        value = -0.5 * both * live_col[rows] * live_row[:, cols]
        if rows == cols:
            value = value + diagonal[rows, cols] * live_col[rows]
        return value * inverse[:, cols]

    def put_start(rows, cols):
        value = halo_start(rows, cols)
        there = slice(ROWS + rows.start, ROWS + rows.stop), slice(ROWS + cols.start, ROWS + cols.stop)
        first_h[there], first_l[there] = split2(value)
        if rows != cols:
            first_h[there[1], there[0]], first_l[there[1], there[0]] = split2(value.T)

    early, late = slice(CUTS[0], CUTS[1]), slice(CUTS[1], CUTS[2])
    for k in range(BLOCKS):
        halo_copy(0, k).wait_recv()
    put_start(early, early)
    for i, j in later:
        if j < COLS - 1:
            acc[kept(i, j)] += square_block(0, span(i), span(j), near)
    for k in range(BLOCKS):
        halo_copy(1, k).wait_recv()
    put_start(early, late)
    put_start(late, late)
    for i, j in later:
        depth = far if j < COLS - 1 else slice(ROWS, M)
        finish(0, 1, i, j, acc[kept(i, j)] + square_block(0, span(i), span(j), depth), scale)

    for number in range(1, ITERS - 1):
        src = number % 2
        weights = step(number)
        for j in range(COLS):
            for i in range(j + 1):
                finish(src, 1 - src, i, j, square_block(src, span(i), span(j), slice(0, M)), weights)

    last = (ITERS - 1) % 2
    scale = step(ITERS - 1)
    for load in load_deriv:
        load.wait()
    for phase in range(2):
        for k in range(BLOCKS):
            halo_copy(phase, k).wait_send()
    zero = jnp.zeros((8, 128), F32)

    def final_block(rows, cols):
        xh, xl = pairs[last]
        old = xh[rows, cols].astype(F32) + xl[rows, cols].astype(F32)
        return scale[0] * old + scale[1] * square_block(last, rows, cols, slice(0, M))

    def put_density(row, col, value):
        height, width = value.shape
        dens_ref[row : row + height, col : col + width] = value
        for side in range(width // 128):
            dens[col // 128 + side, row : row + height] = value[:, side * 128 : (side + 1) * 128]

    def halo_column(q):
        for row in (0, TILE, 2 * TILE):
            value = final_block(slice(row, min(row + TILE, ROWS)), span(q))
            put_density(row, q * TILE, value)
            if q == 2 and row < 2 * TILE:
                put_density(2 * TILE, row, value[:, 0 : ROWS - 2 * TILE].T)

    def core_column(q):
        for i in range(q + 1):
            value = final_block(span(i), span(q))
            put_density(i * TILE, q * TILE, value)
            if i < q:
                put_density(q * TILE, i * TILE, value.T)

    def force_column(q):
        def group(g, sums):
            sums = [list(pair) for pair in sums]
            atoms = slice(g * 8, g * 8 + 8)
            local = [None, None, None]
            for side in range(2):
                lanes = slice(q * TILE + side * 128, q * TILE + (side + 1) * 128)
                rows = [dens[2 * q + side, pl.ds(g * 8 * ORB + mu, 8, stride=ORB)] for mu in range(ORB)]
                for c in range(3):
                    term = rows[0] * dbuf[c, 0, atoms, lanes]
                    for mu in range(1, ORB):
                        term = term + rows[mu] * dbuf[c, mu, atoms, lanes]
                    sums[c][side] = sums[c][side] + term
                    local[c] = term if side == 0 else local[c] + term
            for c in range(3):
                own[c, atoms] += local[c]
            return tuple(tuple(pair) for pair in sums)

        sums = ((zero, zero),) * 3
        for g in range(ATOM_DEV // 8):
            sums = group(g, sums)
        return [[jnp.sum(value, axis=0, keepdims=True) for value in pair] for pair in sums]

    def by_parts(sums):
        for c in range(3):
            rsum[c : c + 1] = jnp.concatenate([piece[c] for piece in sums], axis=1)
        parts = split3(rsum[0:8])
        return jnp.concatenate([p.astype(F32) for p in parts], axis=0).astype(BF16)

    def joined(value):
        return value[0:8] + value[8:16] + value[16:24]

    def halves(triples, which):
        return [t[which] for t in triples]

    halo_column(2)
    halo_column(3)
    two = force_column(2)
    halo_column(4)
    three = force_column(3)
    core_column(0)
    four = force_column(4)
    halo_sums = by_parts([halves(two, 1), halves(three, 0), halves(three, 1), halves(four, 0), halves(four, 1)])
    exchanges = []
    for k in range(BLOCKS):
        terms = -2.0 * joined(mm_nt(halo_sums, select[k]))
        fsend[k, :, 0:ATOM_DEV] = terms
        send = pltpu.make_async_remote_copy(
            src_ref=fsend.at[k],
            dst_ref=frecv.at[k],
            send_sem=fsend_sem.at[k],
            recv_sem=frecv_sem.at[k],
            device_id=(peer(block_offset(k)),),
            device_id_type=MESH,
        )
        send.start()
        exchanges.append(send)
    core_column(1)
    zeroth = force_column(0)
    first = force_column(1)
    core_sums = by_parts([halves(zeroth, 0), halves(zeroth, 1), halves(first, 0), halves(first, 1), halves(two, 0)])
    atom_of_lane = (
        lax.broadcasted_iota(jnp.int32, (ATOM_DEV, ROWS), 1) // ORB
        == lax.broadcasted_iota(jnp.int32, (ATOM_DEV, ROWS), 0)
    ).astype(BF16)
    total = -2.0 * joined(mm_nt(core_sums, atom_of_lane))
    ones = jnp.ones((8, 3 * 128), BF16)
    row_of = lax.broadcasted_iota(jnp.int32, (8, ATOM_DEV), 0)
    for c in range(3):
        parts = jnp.concatenate([p.astype(F32) for p in split3(own[c])], axis=1).astype(BF16)
        total = total + jnp.where(row_of == c, 2.0 * mm_nt(ones, parts), 0.0)
    for exchange in exchanges:
        exchange.wait()
    for k in range(BLOCKS):
        total = total + frecv[k, :, 0:ATOM_DEV]
    force_ref[...] = total[0:3]


def per_device(ham_core, halo_rows, halo_request, deriv, e_low, e_high, branches):
    smem = pl.BlockSpec(memory_space=pltpu.SMEM)
    vmem = pl.BlockSpec(memory_space=pltpu.VMEM)
    hbm = pl.BlockSpec(memory_space=pl.ANY)
    dma = pltpu.SemaphoreType.DMA
    return pl.pallas_call(
        sp2_kernel,
        out_shape=(
            pltpu.VMEM((ROWS, M), F32),
            pltpu.VMEM((3, ATOM_DEV), F32),
        ),
        in_specs=[smem, smem, smem, vmem, hbm, hbm, hbm],
        out_specs=(vmem, vmem),
        scratch_shapes=[
            pltpu.VMEM((ROWS, M), F32),
            pltpu.VMEM((ROWS, ROWS), F32),
            pltpu.VMEM((3, ORB, ATOM_DEV, M), F32),
            pltpu.VMEM((M, M), BF16),
            pltpu.VMEM((M, M), BF16),
            pltpu.VMEM((M, M), BF16),
            pltpu.VMEM((M, M), BF16),
            pltpu.VMEM((M, M - 2 * TILE), F32),
            pltpu.VMEM((2 * COLS, ROWS, 128), F32),
            pltpu.VMEM((3, ATOM_DEV, 128), F32),
            pltpu.VMEM((BLOCKS, ATOM_DEV, ROWS), BF16),
            pltpu.VMEM((8, ROWS), F32),
            pltpu.VMEM((BLOCKS, 8, TILE), F32),
            pltpu.VMEM((BLOCKS, 8, TILE), F32),
            dma((1,)),
            dma((3 * ORB,)),
            dma((2, BLOCKS)),
            dma((2, BLOCKS)),
            dma((BLOCKS,)),
            dma((BLOCKS,)),
        ],
        compiler_params=pltpu.CompilerParams(
            collective_id=0, has_side_effects=True, vmem_limit_bytes=52 << 20
        ),
    )(e_low, e_high, branches, halo_request, ham_core, halo_rows, deriv)


def solution(mesh):
    in_specs = (
        P("dom", None),
        P("dom", None, None, None),
        P("dom", None),
        P(None, "dom", None, None),
        P(),
        P(),
        P(),
    )
    out_specs = (P("dom", None), P(None, "dom"))
    return jax.shard_map(
        per_device, mesh=mesh, in_specs=in_specs, out_specs=out_specs, check_vma=False
    )
```

```python
import jax
import jax.numpy as jnp
from jax import lax
from jax.experimental import pallas as pl
from jax.experimental.pallas import tpu as pltpu
from jax.sharding import PartitionSpec as P

ORB = 4
ATOM_DEV = 160
NB = 4
BLOCKS = 2 * NB
ITERS = 5
ROWS = 640
M = 1280
SLOT_ROWS = ROWS // BLOCKS
TILE = 256
COLS = M // TILE
F32 = jnp.float32
BF16 = jnp.bfloat16
CUTS = (0, 384, 640)
MESH = pl.DeviceIdType.MESH


def block_offset(block):
    if block < NB:
        return block + 1
    return NB - 1 - block


def mm(left, right):
    return jnp.dot(left, right, preferred_element_type=F32)


def mm_nt(left, right):
    return lax.dot_general(left, right, (((1,), (1,)), ((), ())), preferred_element_type=F32)


def span(i):
    return slice(i * TILE, (i + 1) * TILE)


def split2(value):
    high = value.astype(BF16)
    return high, (value - high.astype(F32)).astype(BF16)


def split3(value):
    high = value.astype(BF16)
    rest = value - high.astype(F32)
    mid = rest.astype(BF16)
    return high, mid, (rest - mid.astype(F32)).astype(BF16)


def sp2_kernel(
    low_ref, high_ref, branch_ref, request_ref, ham_ref, halo_ref, deriv_ref,
    dens_ref, force_ref,
    core, halo, dbuf, even_h, even_l, odd_h, odd_l, acc, dens, own, select, rsum, fsend, frecv,
    core_sem, deriv_sem, send_sem, recv_sem, fsend_sem, frecv_sem,
):
    count = lax.axis_size("dom")
    me = lax.axis_index("dom")

    def peer(offset):
        return lax.rem(me + offset + count, count)

    load_core = pltpu.make_async_copy(ham_ref, core, core_sem.at[0])
    load_core.start()
    barrier = pltpu.get_barrier_semaphore()
    for k in range(BLOCKS):
        pl.semaphore_signal(barrier, inc=1, device_id=(peer(block_offset(k)),), device_id_type=MESH)
    pl.semaphore_wait(barrier, BLOCKS)

    def halo_copy(phase, k):
        return pltpu.make_async_remote_copy(
            src_ref=halo_ref.at[0, k, :, ROWS + CUTS[phase] : ROWS + CUTS[phase + 1]],
            dst_ref=halo.at[k * SLOT_ROWS : (k + 1) * SLOT_ROWS, CUTS[phase] : CUTS[phase + 1]],
            send_sem=send_sem.at[phase, k],
            recv_sem=recv_sem.at[phase, k],
            device_id=(peer(-block_offset(k)),),
            device_id_type=MESH,
        )

    on_first = lax.rem(me, 2) == 0

    def send_phase(phase):
        def start(order):
            for k in order:
                halo_copy(phase, k).start()

        pl.when(on_first)(lambda: start((3, 7, 2, 6, 1, 5, 0, 4)))
        pl.when(jnp.logical_not(on_first))(lambda: start((0, 4, 1, 5, 2, 6, 3, 7)))

    send_phase(0)
    request = request_ref[...]
    live = (request >= 0).astype(F32)
    spread_atom = (
        lax.broadcasted_iota(jnp.int32, (ROWS, ATOM_DEV), 0) // ORB
        == lax.broadcasted_iota(jnp.int32, (ROWS, ATOM_DEV), 1)
    ).astype(F32)
    live_col = jnp.sum(spread_atom * live, axis=1, keepdims=True)
    eight = jnp.broadcast_to(live, (8, ATOM_DEV))
    live_row = mm_nt(eight.astype(BF16), spread_atom.astype(BF16))[0:1]
    ids = jnp.broadcast_to(request.astype(F32), (8, ATOM_DEV))
    slot_atom = mm_nt(ids.astype(BF16), spread_atom.astype(BF16))[0:1]
    lane_block = lax.broadcasted_iota(jnp.int32, (1, ROWS), 1) // SLOT_ROWS
    atom_row = lax.broadcasted_iota(jnp.int32, (ATOM_DEV, ROWS), 0).astype(F32)
    for k in range(BLOCKS):
        wanted = jnp.where(lane_block == k, slot_atom, -1.0)
        select[k] = (atom_row == wanted).astype(BF16)
    fsend[...] = jnp.zeros_like(fsend)
    rsum[...] = jnp.zeros_like(rsum)
    own[...] = jnp.zeros_like(own)

    high = high_ref[0]
    inverse = 1.0 / jnp.broadcast_to(high - low_ref[0], (1, ROWS))
    diagonal = (
        lax.broadcasted_iota(jnp.int32, (ROWS, ROWS), 0)
        == lax.broadcasted_iota(jnp.int32, (ROWS, ROWS), 1)
    ).astype(F32) * high

    def step(i):
        taken = branch_ref[i].astype(F32)
        return 2.0 * taken, 1.0 - 2.0 * taken

    pairs = ((even_h, even_l), (odd_h, odd_l))
    first_h, first_l = pairs[0]

    def square_block(src, rows, cols, depth):
        xh, xl = pairs[src]
        left = xh[rows, depth]
        right = xh[depth, cols]
        small = mm(left, xl[depth, cols])
        if rows == cols:
            return mm(left, right) + (small + small.T)
        return mm(left, right) + mm(xl[rows, depth], right) + small

    def finish(src, dst, i, j, square, scale):
        xh, xl = pairs[src]
        yh, yl = pairs[dst]
        old = xh[span(i), span(j)].astype(F32) + xl[span(i), span(j)].astype(F32)
        new = scale[0] * old + scale[1] * square
        yh[span(i), span(j)], yl[span(i), span(j)] = split2(new)
        if i < j:
            yh[span(j), span(i)], yl[span(j), span(i)] = split2(new.T)

    load_core.wait()
    own_part = core[:, 0:ROWS]
    start = (diagonal - 0.5 * (own_part + own_part.T)) * inverse
    h, l = split2(start)
    first_h[0:ROWS, 0:ROWS] = h
    first_l[0:ROWS, 0:ROWS] = l
    cross = -(core[:, ROWS:M] * live_row) * inverse
    h, l = split2(cross)
    first_h[0:ROWS, ROWS:M] = h
    first_l[0:ROWS, ROWS:M] = l
    h, l = split2(cross.T)
    first_h[ROWS:M, 0:ROWS] = h
    first_l[ROWS:M, 0:ROWS] = l
    scale = step(0)
    whole = slice(0, M)
    near = slice(ROWS, ROWS + CUTS[1])
    far = slice(ROWS + CUTS[1], M)
    later = [(i, j) for j in range(2, COLS) for i in range(j + 1)]

    def kept(i, j):
        return span(i), slice(j * TILE - 2 * TILE, (j + 1) * TILE - 2 * TILE)

    for i, j in ((0, 0), (0, 1), (1, 1)):
        finish(0, 1, i, j, square_block(0, span(i), span(j), whole), scale)
    for i, j in later:
        acc[kept(i, j)] = square_block(0, span(i), span(j), slice(0, ROWS))

    def halo_start(rows, cols):
        both = halo[rows, cols] + halo[cols, rows].T
        value = -0.5 * both * live_col[rows] * live_row[:, cols]
        if rows == cols:
            value = value + diagonal[rows, cols] * live_col[rows]
        return value * inverse[:, cols]

    def put_start(rows, cols):
        value = halo_start(rows, cols)
        there = slice(ROWS + rows.start, ROWS + rows.stop), slice(ROWS + cols.start, ROWS + cols.stop)
        first_h[there], first_l[there] = split2(value)
        if rows != cols:
            first_h[there[1], there[0]], first_l[there[1], there[0]] = split2(value.T)

    send_phase(1)
    early, late = slice(CUTS[0], CUTS[1]), slice(CUTS[1], CUTS[2])
    for k in range(BLOCKS):
        halo_copy(0, k).wait_recv()
    put_start(early, early)
    for i, j in later:
        if j < COLS - 1:
            acc[kept(i, j)] += square_block(0, span(i), span(j), near)
    for k in range(BLOCKS):
        halo_copy(1, k).wait_recv()
    load_deriv = []
    for c in range(3):
        for mu in range(ORB):
            load = pltpu.make_async_copy(deriv_ref.at[c, :, mu, :], dbuf.at[c, mu], deriv_sem.at[c * ORB + mu])
            load.start()
            load_deriv.append(load)

    put_start(early, late)
    put_start(late, late)
    for i, j in later:
        depth = far if j < COLS - 1 else slice(ROWS, M)
        finish(0, 1, i, j, acc[kept(i, j)] + square_block(0, span(i), span(j), depth), scale)

    for number in range(1, ITERS - 1):
        src = number % 2
        weights = step(number)
        for j in range(COLS):
            for i in range(j + 1):
                finish(src, 1 - src, i, j, square_block(src, span(i), span(j), slice(0, M)), weights)

    last = (ITERS - 1) % 2
    scale = step(ITERS - 1)
    for load in load_deriv:
        load.wait()
    for phase in range(2):
        for k in range(BLOCKS):
            halo_copy(phase, k).wait_send()
    zero = jnp.zeros((8, 128), F32)

    def final_block(rows, cols):
        xh, xl = pairs[last]
        old = xh[rows, cols].astype(F32) + xl[rows, cols].astype(F32)
        return scale[0] * old + scale[1] * square_block(last, rows, cols, slice(0, M))

    def put_density(row, col, value):
        height, width = value.shape
        dens_ref[row : row + height, col : col + width] = value
        for side in range(width // 128):
            dens[col // 128 + side, row : row + height] = value[:, side * 128 : (side + 1) * 128]

    def halo_column(q):
        for row in (0, TILE, 2 * TILE):
            value = final_block(slice(row, min(row + TILE, ROWS)), span(q))
            put_density(row, q * TILE, value)
            if q == 2 and row < 2 * TILE:
                put_density(2 * TILE, row, value[:, 0 : ROWS - 2 * TILE].T)

    def core_column(q):
        for i in range(q + 1):
            value = final_block(span(i), span(q))
            put_density(i * TILE, q * TILE, value)
            if i < q:
                put_density(q * TILE, i * TILE, value.T)

    def force_column(q):
        def group(g, sums):
            sums = [list(pair) for pair in sums]
            atoms = slice(g * 8, g * 8 + 8)
            local = [None, None, None]
            for side in range(2):
                lanes = slice(q * TILE + side * 128, q * TILE + (side + 1) * 128)
                rows = [dens[2 * q + side, pl.ds(g * 8 * ORB + mu, 8, stride=ORB)] for mu in range(ORB)]
                for c in range(3):
                    term = rows[0] * dbuf[c, 0, atoms, lanes]
                    for mu in range(1, ORB):
                        term = term + rows[mu] * dbuf[c, mu, atoms, lanes]
                    sums[c][side] = sums[c][side] + term
                    local[c] = term if side == 0 else local[c] + term
            for c in range(3):
                own[c, atoms] += local[c]
            return tuple(tuple(pair) for pair in sums)

        sums = ((zero, zero),) * 3
        for g in range(ATOM_DEV // 8):
            sums = group(g, sums)
        return [[jnp.sum(value, axis=0, keepdims=True) for value in pair] for pair in sums]

    def by_parts(sums):
        for c in range(3):
            rsum[c : c + 1] = jnp.concatenate([piece[c] for piece in sums], axis=1)
        parts = split3(rsum[0:8])
        return jnp.concatenate([p.astype(F32) for p in parts], axis=0).astype(BF16)

    def joined(value):
        return value[0:8] + value[8:16] + value[16:24]

    def halves(triples, which):
        return [t[which] for t in triples]

    halo_column(2)
    halo_column(3)
    two = force_column(2)
    halo_column(4)
    three = force_column(3)
    core_column(0)
    four = force_column(4)
    halo_sums = by_parts([halves(two, 1), halves(three, 0), halves(three, 1), halves(four, 0), halves(four, 1)])
    exchanges = []
    for k in range(BLOCKS):
        terms = -2.0 * joined(mm_nt(halo_sums, select[k]))
        fsend[k, :, 0:ATOM_DEV] = terms
        send = pltpu.make_async_remote_copy(
            src_ref=fsend.at[k],
            dst_ref=frecv.at[k],
            send_sem=fsend_sem.at[k],
            recv_sem=frecv_sem.at[k],
            device_id=(peer(block_offset(k)),),
            device_id_type=MESH,
        )
        send.start()
        exchanges.append(send)
    core_column(1)
    zeroth = force_column(0)
    first = force_column(1)
    core_sums = by_parts([halves(zeroth, 0), halves(zeroth, 1), halves(first, 0), halves(first, 1), halves(two, 0)])
    atom_of_lane = (
        lax.broadcasted_iota(jnp.int32, (ATOM_DEV, ROWS), 1) // ORB
        == lax.broadcasted_iota(jnp.int32, (ATOM_DEV, ROWS), 0)
    ).astype(BF16)
    total = -2.0 * joined(mm_nt(core_sums, atom_of_lane))
    ones = jnp.ones((8, 3 * 128), BF16)
    row_of = lax.broadcasted_iota(jnp.int32, (8, ATOM_DEV), 0)
    for c in range(3):
        parts = jnp.concatenate([p.astype(F32) for p in split3(own[c])], axis=1).astype(BF16)
        total = total + jnp.where(row_of == c, 2.0 * mm_nt(ones, parts), 0.0)
    for exchange in exchanges:
        exchange.wait()
    for k in range(BLOCKS):
        total = total + frecv[k, :, 0:ATOM_DEV]
    force_ref[...] = total[0:3]


def per_device(ham_core, halo_rows, halo_request, deriv, e_low, e_high, branches):
    smem = pl.BlockSpec(memory_space=pltpu.SMEM)
    vmem = pl.BlockSpec(memory_space=pltpu.VMEM)
    hbm = pl.BlockSpec(memory_space=pl.ANY)
    dma = pltpu.SemaphoreType.DMA
    return pl.pallas_call(
        sp2_kernel,
        out_shape=(
            pltpu.VMEM((ROWS, M), F32),
            pltpu.VMEM((3, ATOM_DEV), F32),
        ),
        in_specs=[smem, smem, smem, vmem, hbm, hbm, hbm],
        out_specs=(vmem, vmem),
        scratch_shapes=[
            pltpu.VMEM((ROWS, M), F32),
            pltpu.VMEM((ROWS, ROWS), F32),
            pltpu.VMEM((3, ORB, ATOM_DEV, M), F32),
            pltpu.VMEM((M, M), BF16),
            pltpu.VMEM((M, M), BF16),
            pltpu.VMEM((M, M), BF16),
            pltpu.VMEM((M, M), BF16),
            pltpu.VMEM((M, M - 2 * TILE), F32),
            pltpu.VMEM((2 * COLS, ROWS, 128), F32),
            pltpu.VMEM((3, ATOM_DEV, 128), F32),
            pltpu.VMEM((BLOCKS, ATOM_DEV, ROWS), BF16),
            pltpu.VMEM((8, ROWS), F32),
            pltpu.VMEM((BLOCKS, 8, TILE), F32),
            pltpu.VMEM((BLOCKS, 8, TILE), F32),
            dma((1,)),
            dma((3 * ORB,)),
            dma((2, BLOCKS)),
            dma((2, BLOCKS)),
            dma((BLOCKS,)),
            dma((BLOCKS,)),
        ],
        compiler_params=pltpu.CompilerParams(
            collective_id=0, has_side_effects=True, vmem_limit_bytes=52 << 20
        ),
    )(e_low, e_high, branches, halo_request, ham_core, halo_rows, deriv)


def solution(mesh):
    in_specs = (
        P("dom", None),
        P("dom", None, None, None),
        P("dom", None),
        P(None, "dom", None, None),
        P(),
        P(),
        P(),
    )
    out_specs = (P("dom", None), P(None, "dom"))
    return jax.shard_map(
        per_device, mesh=mesh, in_specs=in_specs, out_specs=out_specs, check_vma=False
    )
```

```python
import jax
import jax.numpy as jnp
from jax import lax
from jax.experimental import pallas as pl
from jax.experimental.pallas import tpu as pltpu
from jax.sharding import PartitionSpec as P

ORB = 4
ATOM_DEV = 160
NB = 4
BLOCKS = 2 * NB
ITERS = 5
ROWS = 640
M = 1280
SLOT_ROWS = ROWS // BLOCKS
TILE = 256
COLS = M // TILE
F32 = jnp.float32
BF16 = jnp.bfloat16
CUTS = (0, 384, 640)
MESH = pl.DeviceIdType.MESH


def block_offset(block):
    if block < NB:
        return block + 1
    return NB - 1 - block


def mm(left, right):
    return jnp.dot(left, right, preferred_element_type=F32)


def mm_nt(left, right):
    return lax.dot_general(left, right, (((1,), (1,)), ((), ())), preferred_element_type=F32)


def span(i):
    return slice(i * TILE, (i + 1) * TILE)


def split2(value):
    high = value.astype(BF16)
    return high, (value - high.astype(F32)).astype(BF16)


def split3(value):
    high = value.astype(BF16)
    rest = value - high.astype(F32)
    mid = rest.astype(BF16)
    return high, mid, (rest - mid.astype(F32)).astype(BF16)


def sp2_kernel(
    low_ref, high_ref, branch_ref, request_ref, ham_ref, halo_ref, deriv_ref,
    dens_ref, force_ref,
    core, halo, dbuf, even_h, even_l, odd_h, odd_l, acc, dens, own, select, rsum, fsend, frecv,
    core_sem, deriv_sem, send_sem, recv_sem, fsend_sem, frecv_sem,
):
    count = lax.axis_size("dom")
    me = lax.axis_index("dom")

    def peer(offset):
        return lax.rem(me + offset + count, count)

    load_core = pltpu.make_async_copy(ham_ref, core, core_sem.at[0])
    load_core.start()
    barrier = pltpu.get_barrier_semaphore()
    for k in range(BLOCKS):
        pl.semaphore_signal(barrier, inc=1, device_id=(peer(block_offset(k)),), device_id_type=MESH)
    pl.semaphore_wait(barrier, BLOCKS)

    def halo_copy(phase, k):
        return pltpu.make_async_remote_copy(
            src_ref=halo_ref.at[0, k, :, ROWS + CUTS[phase] : ROWS + CUTS[phase + 1]],
            dst_ref=halo.at[k * SLOT_ROWS : (k + 1) * SLOT_ROWS, CUTS[phase] : CUTS[phase + 1]],
            send_sem=send_sem.at[phase, k],
            recv_sem=recv_sem.at[phase, k],
            device_id=(peer(-block_offset(k)),),
            device_id_type=MESH,
        )

    def start_halo(phase, blocks):
        for k in blocks:
            halo_copy(phase, k).start()

    def sent_halo(phase, blocks):
        for k in blocks:
            halo_copy(phase, k).wait_send()

    distant, close = (3, 7, 2, 6), (1, 5, 0, 4)
    start_halo(0, distant)

    request = request_ref[...]
    live = (request >= 0).astype(F32)
    spread_atom = (
        lax.broadcasted_iota(jnp.int32, (ROWS, ATOM_DEV), 0) // ORB
        == lax.broadcasted_iota(jnp.int32, (ROWS, ATOM_DEV), 1)
    ).astype(F32)
    live_col = jnp.sum(spread_atom * live, axis=1, keepdims=True)
    eight = jnp.broadcast_to(live, (8, ATOM_DEV))
    live_row = mm_nt(eight.astype(BF16), spread_atom.astype(BF16))[0:1]
    ids = jnp.broadcast_to(request.astype(F32), (8, ATOM_DEV))
    slot_atom = mm_nt(ids.astype(BF16), spread_atom.astype(BF16))[0:1]
    lane_block = lax.broadcasted_iota(jnp.int32, (1, ROWS), 1) // SLOT_ROWS
    atom_row = lax.broadcasted_iota(jnp.int32, (ATOM_DEV, ROWS), 0).astype(F32)
    for k in range(BLOCKS):
        wanted = jnp.where(lane_block == k, slot_atom, -1.0)
        select[k] = (atom_row == wanted).astype(BF16)
    fsend[...] = jnp.zeros_like(fsend)
    rsum[...] = jnp.zeros_like(rsum)
    own[...] = jnp.zeros_like(own)

    high = high_ref[0]
    inverse = 1.0 / jnp.broadcast_to(high - low_ref[0], (1, ROWS))
    diagonal = (
        lax.broadcasted_iota(jnp.int32, (ROWS, ROWS), 0)
        == lax.broadcasted_iota(jnp.int32, (ROWS, ROWS), 1)
    ).astype(F32) * high

    def step(i):
        taken = branch_ref[i].astype(F32)
        return 2.0 * taken, 1.0 - 2.0 * taken

    pairs = ((even_h, even_l), (odd_h, odd_l))
    first_h, first_l = pairs[0]

    def square_block(src, rows, cols, depth):
        xh, xl = pairs[src]
        left = xh[rows, depth]
        right = xh[depth, cols]
        small = mm(left, xl[depth, cols])
        if rows == cols:
            return mm(left, right) + (small + small.T)
        return mm(left, right) + mm(xl[rows, depth], right) + small

    def finish(src, dst, i, j, square, scale):
        xh, xl = pairs[src]
        yh, yl = pairs[dst]
        old = xh[span(i), span(j)].astype(F32) + xl[span(i), span(j)].astype(F32)
        new = scale[0] * old + scale[1] * square
        yh[span(i), span(j)], yl[span(i), span(j)] = split2(new)
        if i < j:
            yh[span(j), span(i)], yl[span(j), span(i)] = split2(new.T)

    load_core.wait()
    own_part = core[:, 0:ROWS]
    start = (diagonal - 0.5 * (own_part + own_part.T)) * inverse
    h, l = split2(start)
    first_h[0:ROWS, 0:ROWS] = h
    first_l[0:ROWS, 0:ROWS] = l
    cross = -(core[:, ROWS:M] * live_row) * inverse
    h, l = split2(cross)
    first_h[0:ROWS, ROWS:M] = h
    first_l[0:ROWS, ROWS:M] = l
    h, l = split2(cross.T)
    first_h[ROWS:M, 0:ROWS] = h
    first_l[ROWS:M, 0:ROWS] = l
    scale = step(0)
    whole = slice(0, M)
    near = slice(ROWS, ROWS + CUTS[1])
    far = slice(ROWS + CUTS[1], M)
    later = [(i, j) for j in range(2, COLS) for i in range(j + 1)]

    def kept(i, j):
        return span(i), slice(j * TILE - 2 * TILE, (j + 1) * TILE - 2 * TILE)

    for i, j in ((0, 0), (0, 1), (1, 1)):
        finish(0, 1, i, j, square_block(0, span(i), span(j), whole), scale)
    for i, j in later:
        acc[kept(i, j)] = square_block(0, span(i), span(j), slice(0, ROWS))

    def halo_start(rows, cols):
        both = halo[rows, cols] + halo[cols, rows].T
        value = -0.5 * both * live_col[rows] * live_row[:, cols]
        if rows == cols:
            value = value + diagonal[rows, cols] * live_col[rows]
        return value * inverse[:, cols]

    def put_start(rows, cols):
        value = halo_start(rows, cols)
        there = slice(ROWS + rows.start, ROWS + rows.stop), slice(ROWS + cols.start, ROWS + cols.stop)
        first_h[there], first_l[there] = split2(value)
        if rows != cols:
            first_h[there[1], there[0]], first_l[there[1], there[0]] = split2(value.T)

    sent_halo(0, distant)
    start_halo(0, close)
    start_halo(1, distant)
    early, late = slice(CUTS[0], CUTS[1]), slice(CUTS[1], CUTS[2])
    for k in range(BLOCKS):
        halo_copy(0, k).wait_recv()
    put_start(early, early)
    for i, j in later:
        if j < COLS - 1:
            acc[kept(i, j)] += square_block(0, span(i), span(j), near)
    sent_halo(1, distant)
    start_halo(1, close)
    for k in range(BLOCKS):
        halo_copy(1, k).wait_recv()
    load_deriv = []
    for c in range(3):
        for mu in range(ORB):
            load = pltpu.make_async_copy(deriv_ref.at[c, :, mu, :], dbuf.at[c, mu], deriv_sem.at[c * ORB + mu])
            load.start()
            load_deriv.append(load)

    put_start(early, late)
    put_start(late, late)
    for i, j in later:
        depth = far if j < COLS - 1 else slice(ROWS, M)
        finish(0, 1, i, j, acc[kept(i, j)] + square_block(0, span(i), span(j), depth), scale)

    for number in range(1, ITERS - 1):
        src = number % 2
        weights = step(number)
        for j in range(COLS):
            for i in range(j + 1):
                finish(src, 1 - src, i, j, square_block(src, span(i), span(j), slice(0, M)), weights)

    last = (ITERS - 1) % 2
    scale = step(ITERS - 1)
    for load in load_deriv:
        load.wait()
    sent_halo(0, close)
    sent_halo(1, close)
    zero = jnp.zeros((8, 128), F32)

    def final_block(rows, cols):
        xh, xl = pairs[last]
        old = xh[rows, cols].astype(F32) + xl[rows, cols].astype(F32)
        return scale[0] * old + scale[1] * square_block(last, rows, cols, slice(0, M))

    def put_density(row, col, value):
        height, width = value.shape
        dens_ref[row : row + height, col : col + width] = value
        for side in range(width // 128):
            dens[col // 128 + side, row : row + height] = value[:, side * 128 : (side + 1) * 128]

    def halo_column(q):
        for row in (0, TILE, 2 * TILE):
            value = final_block(slice(row, min(row + TILE, ROWS)), span(q))
            put_density(row, q * TILE, value)
            if q == 2 and row < 2 * TILE:
                put_density(2 * TILE, row, value[:, 0 : ROWS - 2 * TILE].T)

    def core_column(q):
        for i in range(q + 1):
            value = final_block(span(i), span(q))
            put_density(i * TILE, q * TILE, value)
            if i < q:
                put_density(q * TILE, i * TILE, value.T)

    def force_column(q):
        def group(g, sums):
            sums = [list(pair) for pair in sums]
            atoms = slice(g * 8, g * 8 + 8)
            local = [None, None, None]
            for side in range(2):
                lanes = slice(q * TILE + side * 128, q * TILE + (side + 1) * 128)
                rows = [dens[2 * q + side, pl.ds(g * 8 * ORB + mu, 8, stride=ORB)] for mu in range(ORB)]
                for c in range(3):
                    term = rows[0] * dbuf[c, 0, atoms, lanes]
                    for mu in range(1, ORB):
                        term = term + rows[mu] * dbuf[c, mu, atoms, lanes]
                    sums[c][side] = sums[c][side] + term
                    local[c] = term if side == 0 else local[c] + term
            for c in range(3):
                own[c, atoms] += local[c]
            return tuple(tuple(pair) for pair in sums)

        sums = ((zero, zero),) * 3
        for g in range(ATOM_DEV // 8):
            sums = group(g, sums)
        return [[jnp.sum(value, axis=0, keepdims=True) for value in pair] for pair in sums]

    def by_parts(sums):
        for c in range(3):
            rsum[c : c + 1] = jnp.concatenate([piece[c] for piece in sums], axis=1)
        parts = split3(rsum[0:8])
        return jnp.concatenate([p.astype(F32) for p in parts], axis=0).astype(BF16)

    def joined(value):
        return value[0:8] + value[8:16] + value[16:24]

    def halves(triples, which):
        return [t[which] for t in triples]

    halo_column(2)
    halo_column(3)
    two = force_column(2)
    halo_column(4)
    three = force_column(3)
    four = force_column(4)
    halo_sums = by_parts([halves(two, 1), halves(three, 0), halves(three, 1), halves(four, 0), halves(four, 1)])
    exchanges = []
    for k in range(BLOCKS):
        terms = -2.0 * joined(mm_nt(halo_sums, select[k]))
        fsend[k, :, 0:ATOM_DEV] = terms
        send = pltpu.make_async_remote_copy(
            src_ref=fsend.at[k],
            dst_ref=frecv.at[k],
            send_sem=fsend_sem.at[k],
            recv_sem=frecv_sem.at[k],
            device_id=(peer(block_offset(k)),),
            device_id_type=MESH,
        )
        send.start()
        exchanges.append(send)
    core_column(0)
    core_column(1)
    zeroth = force_column(0)
    first = force_column(1)
    core_sums = by_parts([halves(zeroth, 0), halves(zeroth, 1), halves(first, 0), halves(first, 1), halves(two, 0)])
    atom_of_lane = (
        lax.broadcasted_iota(jnp.int32, (ATOM_DEV, ROWS), 1) // ORB
        == lax.broadcasted_iota(jnp.int32, (ATOM_DEV, ROWS), 0)
    ).astype(BF16)
    total = -2.0 * joined(mm_nt(core_sums, atom_of_lane))
    ones = jnp.ones((8, 3 * 128), BF16)
    row_of = lax.broadcasted_iota(jnp.int32, (8, ATOM_DEV), 0)
    for c in range(3):
        parts = jnp.concatenate([p.astype(F32) for p in split3(own[c])], axis=1).astype(BF16)
        total = total + jnp.where(row_of == c, 2.0 * mm_nt(ones, parts), 0.0)
    for exchange in exchanges:
        exchange.wait()
    for k in range(BLOCKS):
        total = total + frecv[k, :, 0:ATOM_DEV]
    force_ref[...] = total[0:3]


def per_device(ham_core, halo_rows, halo_request, deriv, e_low, e_high, branches):
    smem = pl.BlockSpec(memory_space=pltpu.SMEM)
    vmem = pl.BlockSpec(memory_space=pltpu.VMEM)
    hbm = pl.BlockSpec(memory_space=pl.ANY)
    dma = pltpu.SemaphoreType.DMA
    return pl.pallas_call(
        sp2_kernel,
        out_shape=(
            pltpu.VMEM((ROWS, M), F32),
            pltpu.VMEM((3, ATOM_DEV), F32),
        ),
        in_specs=[smem, smem, smem, vmem, hbm, hbm, hbm],
        out_specs=(vmem, vmem),
        scratch_shapes=[
            pltpu.VMEM((ROWS, M), F32),
            pltpu.VMEM((ROWS, ROWS), F32),
            pltpu.VMEM((3, ORB, ATOM_DEV, M), F32),
            pltpu.VMEM((M, M), BF16),
            pltpu.VMEM((M, M), BF16),
            pltpu.VMEM((M, M), BF16),
            pltpu.VMEM((M, M), BF16),
            pltpu.VMEM((M, M - 2 * TILE), F32),
            pltpu.VMEM((2 * COLS, ROWS, 128), F32),
            pltpu.VMEM((3, ATOM_DEV, 128), F32),
            pltpu.VMEM((BLOCKS, ATOM_DEV, ROWS), BF16),
            pltpu.VMEM((8, ROWS), F32),
            pltpu.VMEM((BLOCKS, 8, TILE), F32),
            pltpu.VMEM((BLOCKS, 8, TILE), F32),
            dma((1,)),
            dma((3 * ORB,)),
            dma((2, BLOCKS)),
            dma((2, BLOCKS)),
            dma((BLOCKS,)),
            dma((BLOCKS,)),
        ],
        compiler_params=pltpu.CompilerParams(
            collective_id=0, has_side_effects=True, vmem_limit_bytes=52 << 20
        ),
    )(e_low, e_high, branches, halo_request, ham_core, halo_rows, deriv)


def solution(mesh):
    in_specs = (
        P("dom", None),
        P("dom", None, None, None),
        P("dom", None),
        P(None, "dom", None, None),
        P(),
        P(),
        P(),
    )
    out_specs = (P("dom", None), P(None, "dom"))
    return jax.shard_map(
        per_device, mesh=mesh, in_specs=in_specs, out_specs=out_specs, check_vma=False
    )
```

```python
import jax
import jax.numpy as jnp
from jax import lax
from jax.experimental import pallas as pl
from jax.experimental.pallas import tpu as pltpu
from jax.sharding import PartitionSpec as P

ORB = 4
ATOM_DEV = 160
NB = 4
BLOCKS = 2 * NB
ITERS = 5
ROWS = 640
M = 1280
SLOT_ROWS = ROWS // BLOCKS
TILE = 256
COLS = M // TILE
F32 = jnp.float32
BF16 = jnp.bfloat16
CUTS = (0, 384, 640)
MESH = pl.DeviceIdType.MESH


def block_offset(block):
    if block < NB:
        return block + 1
    return NB - 1 - block


def mm(left, right):
    return jnp.dot(left, right, preferred_element_type=F32)


def mm_nt(left, right):
    return lax.dot_general(left, right, (((1,), (1,)), ((), ())), preferred_element_type=F32)


def span(i):
    return slice(i * TILE, (i + 1) * TILE)


def split2(value):
    high = value.astype(BF16)
    return high, (value - high.astype(F32)).astype(BF16)


def split3(value):
    high = value.astype(BF16)
    rest = value - high.astype(F32)
    mid = rest.astype(BF16)
    return high, mid, (rest - mid.astype(F32)).astype(BF16)


def sp2_kernel(
    low_ref, high_ref, branch_ref, request_ref, ham_ref, halo_ref, deriv_ref,
    dens_ref, force_ref,
    core, halo, dbuf, even_h, even_l, odd_h, odd_l, acc, dens, own, select, rsum, fsend, frecv,
    core_sem, deriv_sem, send_sem, recv_sem, fsend_sem, frecv_sem,
):
    count = lax.axis_size("dom")
    me = lax.axis_index("dom")

    def peer(offset):
        return lax.rem(me + offset + count, count)

    load_core = pltpu.make_async_copy(ham_ref, core, core_sem.at[0])
    load_core.start()
    barrier = pltpu.get_barrier_semaphore()
    for k in range(BLOCKS):
        pl.semaphore_signal(barrier, inc=1, device_id=(peer(block_offset(k)),), device_id_type=MESH)
    pl.semaphore_wait(barrier, BLOCKS)

    def halo_copy(phase, k):
        return pltpu.make_async_remote_copy(
            src_ref=halo_ref.at[0, k, :, ROWS + CUTS[phase] : ROWS + CUTS[phase + 1]],
            dst_ref=halo.at[k * SLOT_ROWS : (k + 1) * SLOT_ROWS, CUTS[phase] : CUTS[phase + 1]],
            send_sem=send_sem.at[phase, k],
            recv_sem=recv_sem.at[phase, k],
            device_id=(peer(-block_offset(k)),),
            device_id_type=MESH,
        )

    def start_halo(phase, blocks):
        for k in blocks:
            halo_copy(phase, k).start()

    def sent_halo(phase, blocks):
        for k in blocks:
            halo_copy(phase, k).wait_send()

    distant, close = (3, 7, 2, 6), (1, 5, 0, 4)
    start_halo(0, distant)

    request = request_ref[...]
    live = (request >= 0).astype(F32)
    spread_atom = (
        lax.broadcasted_iota(jnp.int32, (ROWS, ATOM_DEV), 0) // ORB
        == lax.broadcasted_iota(jnp.int32, (ROWS, ATOM_DEV), 1)
    ).astype(F32)
    live_col = jnp.sum(spread_atom * live, axis=1, keepdims=True)
    eight = jnp.broadcast_to(live, (8, ATOM_DEV))
    live_row = mm_nt(eight.astype(BF16), spread_atom.astype(BF16))[0:1]
    ids = jnp.broadcast_to(request.astype(F32), (8, ATOM_DEV))
    slot_atom = mm_nt(ids.astype(BF16), spread_atom.astype(BF16))[0:1]
    lane_block = lax.broadcasted_iota(jnp.int32, (1, ROWS), 1) // SLOT_ROWS
    atom_row = lax.broadcasted_iota(jnp.int32, (ATOM_DEV, ROWS), 0).astype(F32)
    for k in range(BLOCKS):
        wanted = jnp.where(lane_block == k, slot_atom, -1.0)
        select[k] = (atom_row == wanted).astype(BF16)
    fsend[...] = jnp.zeros_like(fsend)
    rsum[...] = jnp.zeros_like(rsum)
    own[...] = jnp.zeros_like(own)

    high = high_ref[0]
    inverse = 1.0 / jnp.broadcast_to(high - low_ref[0], (1, ROWS))
    diagonal = (
        lax.broadcasted_iota(jnp.int32, (ROWS, ROWS), 0)
        == lax.broadcasted_iota(jnp.int32, (ROWS, ROWS), 1)
    ).astype(F32) * high

    def step(i):
        taken = branch_ref[i].astype(F32)
        return 2.0 * taken, 1.0 - 2.0 * taken

    pairs = ((even_h, even_l), (odd_h, odd_l))
    first_h, first_l = pairs[0]

    def square_block(src, rows, cols, depth):
        xh, xl = pairs[src]
        left = xh[rows, depth]
        right = xh[depth, cols]
        small = mm(left, xl[depth, cols])
        if rows == cols:
            return mm(left, right) + (small + small.T)
        return mm(left, right) + mm(xl[rows, depth], right) + small

    def finish(src, dst, i, j, square, scale):
        xh, xl = pairs[src]
        yh, yl = pairs[dst]
        old = xh[span(i), span(j)].astype(F32) + xl[span(i), span(j)].astype(F32)
        new = scale[0] * old + scale[1] * square
        yh[span(i), span(j)], yl[span(i), span(j)] = split2(new)
        if i < j:
            yh[span(j), span(i)], yl[span(j), span(i)] = split2(new.T)

    load_core.wait()
    own_part = core[:, 0:ROWS]
    start = (diagonal - 0.5 * (own_part + own_part.T)) * inverse
    h, l = split2(start)
    first_h[0:ROWS, 0:ROWS] = h
    first_l[0:ROWS, 0:ROWS] = l
    cross = -(core[:, ROWS:M] * live_row) * inverse
    h, l = split2(cross)
    first_h[0:ROWS, ROWS:M] = h
    first_l[0:ROWS, ROWS:M] = l
    h, l = split2(cross.T)
    first_h[ROWS:M, 0:ROWS] = h
    first_l[ROWS:M, 0:ROWS] = l
    scale = step(0)
    whole = slice(0, M)
    near = slice(ROWS, ROWS + CUTS[1])
    far = slice(ROWS + CUTS[1], M)
    later = [(i, j) for j in range(2, COLS) for i in range(j + 1)]

    def kept(i, j):
        return span(i), slice(j * TILE - 2 * TILE, (j + 1) * TILE - 2 * TILE)

    for i, j in ((0, 0), (0, 1), (1, 1)):
        finish(0, 1, i, j, square_block(0, span(i), span(j), whole), scale)
    sent_halo(0, distant)
    start_halo(0, close)
    start_halo(1, distant)
    for i, j in later:
        acc[kept(i, j)] = square_block(0, span(i), span(j), slice(0, ROWS))

    def halo_start(rows, cols):
        both = halo[rows, cols] + halo[cols, rows].T
        value = -0.5 * both * live_col[rows] * live_row[:, cols]
        if rows == cols:
            value = value + diagonal[rows, cols] * live_col[rows]
        return value * inverse[:, cols]

    def put_start(rows, cols):
        value = halo_start(rows, cols)
        there = slice(ROWS + rows.start, ROWS + rows.stop), slice(ROWS + cols.start, ROWS + cols.stop)
        first_h[there], first_l[there] = split2(value)
        if rows != cols:
            first_h[there[1], there[0]], first_l[there[1], there[0]] = split2(value.T)

    early, late = slice(CUTS[0], CUTS[1]), slice(CUTS[1], CUTS[2])
    for k in range(BLOCKS):
        halo_copy(0, k).wait_recv()
    sent_halo(1, distant)
    start_halo(1, close)
    put_start(early, early)
    for i, j in later:
        if j < COLS - 1:
            acc[kept(i, j)] += square_block(0, span(i), span(j), near)
    for k in range(BLOCKS):
        halo_copy(1, k).wait_recv()
    load_deriv = []
    for c in range(3):
        for mu in range(ORB):
            load = pltpu.make_async_copy(deriv_ref.at[c, :, mu, :], dbuf.at[c, mu], deriv_sem.at[c * ORB + mu])
            load.start()
            load_deriv.append(load)

    put_start(early, late)
    put_start(late, late)
    for i, j in later:
        depth = far if j < COLS - 1 else slice(ROWS, M)
        finish(0, 1, i, j, acc[kept(i, j)] + square_block(0, span(i), span(j), depth), scale)

    for number in range(1, ITERS - 1):
        src = number % 2
        weights = step(number)
        for j in range(COLS):
            for i in range(j + 1):
                finish(src, 1 - src, i, j, square_block(src, span(i), span(j), slice(0, M)), weights)

    last = (ITERS - 1) % 2
    scale = step(ITERS - 1)
    for load in load_deriv:
        load.wait()
    sent_halo(0, close)
    sent_halo(1, close)
    zero = jnp.zeros((8, 128), F32)

    def final_block(rows, cols):
        xh, xl = pairs[last]
        old = xh[rows, cols].astype(F32) + xl[rows, cols].astype(F32)
        return scale[0] * old + scale[1] * square_block(last, rows, cols, slice(0, M))

    def put_density(row, col, value):
        height, width = value.shape
        dens_ref[row : row + height, col : col + width] = value
        for side in range(width // 128):
            dens[col // 128 + side, row : row + height] = value[:, side * 128 : (side + 1) * 128]

    def halo_column(q):
        for row in (0, TILE, 2 * TILE):
            value = final_block(slice(row, min(row + TILE, ROWS)), span(q))
            put_density(row, q * TILE, value)
            if q == 2 and row < 2 * TILE:
                put_density(2 * TILE, row, value[:, 0 : ROWS - 2 * TILE].T)

    def core_column(q):
        for i in range(q + 1):
            value = final_block(span(i), span(q))
            put_density(i * TILE, q * TILE, value)
            if i < q:
                put_density(q * TILE, i * TILE, value.T)

    def force_column(q):
        def group(g, sums):
            sums = [list(pair) for pair in sums]
            atoms = slice(g * 8, g * 8 + 8)
            local = [None, None, None]
            for side in range(2):
                lanes = slice(q * TILE + side * 128, q * TILE + (side + 1) * 128)
                rows = [dens[2 * q + side, pl.ds(g * 8 * ORB + mu, 8, stride=ORB)] for mu in range(ORB)]
                for c in range(3):
                    term = rows[0] * dbuf[c, 0, atoms, lanes]
                    for mu in range(1, ORB):
                        term = term + rows[mu] * dbuf[c, mu, atoms, lanes]
                    sums[c][side] = sums[c][side] + term
                    local[c] = term if side == 0 else local[c] + term
            for c in range(3):
                own[c, atoms] += local[c]
            return tuple(tuple(pair) for pair in sums)

        sums = ((zero, zero),) * 3
        for g in range(ATOM_DEV // 8):
            sums = group(g, sums)
        return [[jnp.sum(value, axis=0, keepdims=True) for value in pair] for pair in sums]

    def by_parts(sums):
        for c in range(3):
            rsum[c : c + 1] = jnp.concatenate([piece[c] for piece in sums], axis=1)
        parts = split3(rsum[0:8])
        return jnp.concatenate([p.astype(F32) for p in parts], axis=0).astype(BF16)

    def joined(value):
        return value[0:8] + value[8:16] + value[16:24]

    def halves(triples, which):
        return [t[which] for t in triples]

    halo_column(2)
    halo_column(3)
    two = force_column(2)
    halo_column(4)
    three = force_column(3)
    four = force_column(4)
    halo_sums = by_parts([halves(two, 1), halves(three, 0), halves(three, 1), halves(four, 0), halves(four, 1)])
    exchanges = []
    for k in range(BLOCKS):
        terms = -2.0 * joined(mm_nt(halo_sums, select[k]))
        fsend[k, :, 0:ATOM_DEV] = terms
        send = pltpu.make_async_remote_copy(
            src_ref=fsend.at[k],
            dst_ref=frecv.at[k],
            send_sem=fsend_sem.at[k],
            recv_sem=frecv_sem.at[k],
            device_id=(peer(block_offset(k)),),
            device_id_type=MESH,
        )
        send.start()
        exchanges.append(send)
    core_column(0)
    core_column(1)
    zeroth = force_column(0)
    first = force_column(1)
    core_sums = by_parts([halves(zeroth, 0), halves(zeroth, 1), halves(first, 0), halves(first, 1), halves(two, 0)])
    atom_of_lane = (
        lax.broadcasted_iota(jnp.int32, (ATOM_DEV, ROWS), 1) // ORB
        == lax.broadcasted_iota(jnp.int32, (ATOM_DEV, ROWS), 0)
    ).astype(BF16)
    total = -2.0 * joined(mm_nt(core_sums, atom_of_lane))
    ones = jnp.ones((8, 3 * 128), BF16)
    row_of = lax.broadcasted_iota(jnp.int32, (8, ATOM_DEV), 0)
    for c in range(3):
        parts = jnp.concatenate([p.astype(F32) for p in split3(own[c])], axis=1).astype(BF16)
        total = total + jnp.where(row_of == c, 2.0 * mm_nt(ones, parts), 0.0)
    for exchange in exchanges:
        exchange.wait()
    for k in range(BLOCKS):
        total = total + frecv[k, :, 0:ATOM_DEV]
    force_ref[...] = total[0:3]


def per_device(ham_core, halo_rows, halo_request, deriv, e_low, e_high, branches):
    smem = pl.BlockSpec(memory_space=pltpu.SMEM)
    vmem = pl.BlockSpec(memory_space=pltpu.VMEM)
    hbm = pl.BlockSpec(memory_space=pl.ANY)
    dma = pltpu.SemaphoreType.DMA
    return pl.pallas_call(
        sp2_kernel,
        out_shape=(
            pltpu.VMEM((ROWS, M), F32),
            pltpu.VMEM((3, ATOM_DEV), F32),
        ),
        in_specs=[smem, smem, smem, vmem, hbm, hbm, hbm],
        out_specs=(vmem, vmem),
        scratch_shapes=[
            pltpu.VMEM((ROWS, M), F32),
            pltpu.VMEM((ROWS, ROWS), F32),
            pltpu.VMEM((3, ORB, ATOM_DEV, M), F32),
            pltpu.VMEM((M, M), BF16),
            pltpu.VMEM((M, M), BF16),
            pltpu.VMEM((M, M), BF16),
            pltpu.VMEM((M, M), BF16),
            pltpu.VMEM((M, M - 2 * TILE), F32),
            pltpu.VMEM((2 * COLS, ROWS, 128), F32),
            pltpu.VMEM((3, ATOM_DEV, 128), F32),
            pltpu.VMEM((BLOCKS, ATOM_DEV, ROWS), BF16),
            pltpu.VMEM((8, ROWS), F32),
            pltpu.VMEM((BLOCKS, 8, TILE), F32),
            pltpu.VMEM((BLOCKS, 8, TILE), F32),
            dma((1,)),
            dma((3 * ORB,)),
            dma((2, BLOCKS)),
            dma((2, BLOCKS)),
            dma((BLOCKS,)),
            dma((BLOCKS,)),
        ],
        compiler_params=pltpu.CompilerParams(
            collective_id=0, has_side_effects=True, vmem_limit_bytes=52 << 20
        ),
    )(e_low, e_high, branches, halo_request, ham_core, halo_rows, deriv)


def solution(mesh):
    in_specs = (
        P("dom", None),
        P("dom", None, None, None),
        P("dom", None),
        P(None, "dom", None, None),
        P(),
        P(),
        P(),
    )
    out_specs = (P("dom", None), P(None, "dom"))
    return jax.shard_map(
        per_device, mesh=mesh, in_specs=in_specs, out_specs=out_specs, check_vma=False
    )
```
